256 devices in a mesh: gx: 16 (over y, x), gy: 16 (over z, core).
Axes of the slice: x: 4, y: 4, z: 8, core: 2. Of those that a mesh axis runs over, the one named last changes fastest.
Arguments:
- rhs: bfloat16 [2048, 384, 128], P(('gx', 'gy')), may hold values from -6 to 6
- diag_blocks: bfloat16 [2048, 384, 384], P(('gx', 'gy'))
- inverse_blocks: bfloat16 [2048, 384, 384], P(('gx', 'gy'))
- couplings: bfloat16 [2048, 6, 384, 96], P(('gx', 'gy')), may hold values from -0.25 to 0.25
- prolong: bfloat16 [384, 48], replicated, may hold values from -0.3125 to 0.3125
- face_source: int32 [2048, 6], P(('gx', 'gy')), may hold values from 0 to 5, as said below
- subset: int32 [2048], P(('gx', 'gy')), may hold values from 0 to 15
Outputs:
- solution: float32 [2048, 384, 128], P(('gx', 'gy'))
The draws below stay inside these ranges and needn't reach their ends.
Inputs may be any that keep to these rules, and one draw needn't show every extreme that they name: `face_source`: face f of an element and face f xor 1 of its neighbour are both boundary faces or both not. A face that is not a boundary face has code 1 where its neighbour lies inside the same partition and the code of its direction otherwise; face 4 at k = 0 and face 5 at k = 1 are boundary faces. `subset`: subsets of different rows of partitions are different.
All inputs are finite; a program needn't handle non-finite values.
Results may differ from the reference program's by a relative error of at most 0.0055.
Values may be sent and summed in bfloat16 or wider, within the bound.
A program may use at most 64 MiB of HBM per device.

```python
import math
import jax
import jax.numpy as jnp
import numpy as np
from jax import lax

NVAR = 6
NP = 4
NRHS = 128
EZ = 2
CITER = 4
E_DEV = 8
DOF = 384
FDOF = 96
CDOF = 48
ELEMS = 2048
SUBS = 16
N_GX = 16
N_GY = 16


def draw_block_set(key):
    noise = jax.random.normal(key, (ELEMS, DOF, DOF), jnp.float32)
    blocks = jnp.eye(DOF, dtype=jnp.float32)[None] + noise * (0.3 / math.sqrt(DOF))
    return blocks.astype(jnp.bfloat16)


def draw_diag_blocks(key, part):
    return draw_block_set(jax.random.fold_in(key, 11))


def draw_inverse_blocks(key, part):
    return draw_block_set(jax.random.fold_in(key, 23))


def draw_face_source(key, part):
    cells_x = 2 * N_GX
    cells_y = 2 * N_GY
    open_x = jax.random.randint(jax.random.fold_in(key, 5), (cells_x, cells_y, EZ), 0, 8) > 0
    open_y = jax.random.randint(jax.random.fold_in(key, 7), (cells_x, cells_y, EZ), 0, 8) > 0
    element = jnp.arange(ELEMS, dtype=jnp.int32)
    device = element // E_DEV
    local = element % E_DEV
    row_pos = device // N_GY
    col_pos = device % N_GY
    place_i = local % 2
    place_j = local // 2 % 2
    place_k = local // 4
    cell_x = row_pos * 2 + place_i
    cell_y = col_pos * 2 + place_j
    live0 = open_x[(cell_x - 1) % cells_x, cell_y, place_k]
    live1 = open_x[cell_x, cell_y, place_k]
    live2 = open_y[cell_x, (cell_y - 1) % cells_y, place_k]
    live3 = open_y[cell_x, cell_y, place_k]
    live4 = place_k > 0
    live5 = place_k < EZ - 1
    code0 = jnp.where(place_i == 1, 1, 2)
    code1 = jnp.where(place_i == 0, 1, 3)
    code2 = jnp.where(place_j == 1, 1, 4)
    code3 = jnp.where(place_j == 0, 1, 5)
    ones = jnp.ones_like(local)
    lives = [live0, live1, live2, live3, live4, live5]
    codes = [code0, code1, code2, code3, ones, ones]
    columns = [jnp.where(lives[index], codes[index], 0) for index in range(6)]
    return jnp.stack(columns, axis=1).astype(jnp.int32)


def touch_ends(drawn, key, low, top_value):
    dims = drawn.shape
    spot = [jax.random.randint(jax.random.fold_in(key, axis), (), 0, dims[axis]) for axis in range(len(dims))]
    drawn = drawn.at[tuple(spot)].set(low)
    longest = dims.index(max(dims))
    spot[longest] = (spot[longest] + 1) % dims[longest]
    return drawn.at[tuple(spot)].set(top_value)


def block_levels(key, dims, pieces, low, top_value):
    factor_of = 1.0
    for position, parts in pieces:
        steps = jax.random.uniform(jax.random.fold_in(jax.random.fold_in(key, 6), position), (parts,), jnp.float32, low / len(pieces), top_value / len(pieces))
        factor_of = factor_of * jnp.repeat(jnp.exp(steps), dims[position] // parts).reshape((-1,) + (1,) * (len(dims) - 1 - position))
    return factor_of


def rank_bounds(number_of, lean):
    loads = [(1 << 20) // math.isqrt(standing ** lean) + 1 for standing in range(1, number_of + 1)]
    spread = 1 + sum(loads) // (1 << 30)
    return np.cumsum(np.array([max(1, weight // spread) for weight in loads]))


def ranked_ids(own_key, shape, number_of, skew):
    grid = rank_bounds(number_of, skew)
    ticket = jax.random.randint(jax.random.fold_in(own_key, 1), shape, 0, int(grid[number_of - 1]))
    rank = jnp.searchsorted(jnp.asarray(grid, jnp.int32), ticket, side="right")
    return jax.random.permutation(jax.random.fold_in(own_key, 2), number_of)[rank].astype(jnp.int32)


def scatter_about(own_key, shape, scale, reach, cuts=(), held_as=jnp.bfloat16):
    loudness = block_levels(own_key, shape, cuts, -0.22, 0.18) if cuts else 1.0
    values = jax.random.normal(own_key, shape, jnp.float32) * scale * loudness
    return jnp.minimum(jnp.maximum(values, -reach), reach).astype(held_as)


def setup_inputs(seed: int = 0) -> dict:
    seeds = jax.random.split(jax.random.key(seed), 8)
    return {
        "rhs": scatter_about(seeds[0], (ELEMS, DOF, NRHS), 1.0, 6.0, ((0, 256),)),
        "diag_blocks": draw_diag_blocks(jax.random.fold_in(seeds[7], 71), 0),
        "inverse_blocks": draw_inverse_blocks(jax.random.fold_in(seeds[7], 71), 0),
        "couplings": scatter_about(seeds[3], (ELEMS, 6, DOF, FDOF), (6 * FDOF) ** -0.5, 0.25, ((0, 256),)),
        "prolong": scatter_about(seeds[4], (DOF, CDOF), DOF ** -0.5, 0.3125),
        "face_source": draw_face_source(jax.random.fold_in(seeds[7], 71), 0),
        "subset": touch_ends(ranked_ids(seeds[6], (ELEMS,), SUBS, 2), jax.random.fold_in(seeds[6], 3), 0, SUBS - 1).astype(jnp.int32),
    }


def face_trace(values, face_id):
    leading = values.shape[0]
    columns = values.shape[-1]
    volume = values.reshape(leading, NVAR, NP, NP, NP, columns)
    sliced = lax.index_in_dim(volume, (NP - 1) * (face_id % 2), 4 - face_id // 2, keepdims=False)
    return sliced.reshape(leading, NVAR * NP * NP, columns)


def blockwise(function, arrays):
    blocks = ELEMS // E_DEV
    split = tuple(array_item.reshape((blocks, E_DEV) + array_item.shape[1:]) for array_item in arrays)
    result = lax.map(lambda items: function(*items), split)
    return result.reshape((ELEMS,) + result.shape[2:])


def neighbour_ids(face_source):
    element = jnp.arange(ELEMS, dtype=jnp.int32)
    device = element // E_DEV
    local = element % E_DEV
    row_pos = device // N_GY
    col_pos = device % N_GY
    row_shift = jnp.array([0, 0, -1, 1, 0, 0], dtype=jnp.int32)
    col_shift = jnp.array([0, 0, 0, 0, -1, 1], dtype=jnp.int32)
    flips = jnp.array([1, 1, 2, 2, 0, 0], dtype=jnp.int32)
    layer_step = jnp.array([0, 0, 0, 0, -4, 4], dtype=jnp.int32)
    near_local = jnp.clip(jnp.bitwise_xor(local[:, None], flips[None, :]) + layer_step[None, :], 0, E_DEV - 1)
    target_row = (row_pos[:, None] + row_shift[face_source]) % N_GX
    target_col = (col_pos[:, None] + col_shift[face_source]) % N_GY
    return ((target_row * N_GY + target_col) * E_DEV + near_local).astype(jnp.int32)


def batch_diag(blocks, state_b):
    return jnp.einsum("edk,ekr->edr", blocks.astype(jnp.float32), state_b.astype(jnp.float32))


def batch_faces(couplings, near):
    return jnp.einsum("efdt,eftr->edr", couplings.astype(jnp.float32), near.astype(jnp.float32))


def residual_of(state, rhs, diag_blocks, couplings, neighbours, live):
    state_b = state.astype(jnp.bfloat16)
    traces = jnp.stack([face_trace(state_b, face_id) for face_id in range(6)], axis=1)
    near = jnp.stack([traces[:, face_id ^ 1][neighbours[:, face_id]] for face_id in range(6)], axis=1)
    near = jnp.where(live[:, :, None, None], near, jnp.zeros_like(near))
    local_part = blockwise(batch_diag, (diag_blocks, state_b))
    remote_part = blockwise(batch_faces, (couplings, near))
    return rhs.astype(jnp.float32) - local_part - remote_part


def reference(rhs, diag_blocks, inverse_blocks, couplings, prolong, face_source, subset):
    neighbours = neighbour_ids(face_source)
    live = face_source > 0
    first = 0.7 * blockwise(batch_diag, (inverse_blocks, rhs))
    resid = residual_of(first, rhs, diag_blocks, couplings, neighbours, live)
    resid_b = resid.astype(jnp.bfloat16)
    prolong_f = prolong.astype(jnp.float32)
    restricted = jnp.einsum("dc,edr->ecr", prolong_f, resid_b.astype(jnp.float32))
    face_rows = jnp.stack([face_trace(prolong[None], face_id ^ 1)[0] for face_id in range(6)], axis=0)
    masked_rows = jnp.where(live[:, :, None, None], face_rows[None], jnp.zeros_like(face_rows[None]))

    def stiff_block(blocks, coupled, rows):
        inner = jnp.einsum("edk,kc->edc", blocks.astype(jnp.float32), prolong_f)
        outer = jnp.einsum("efdt,eftc->edc", coupled.astype(jnp.float32), rows.astype(jnp.float32))
        return inner + outer

    stiff = blockwise(stiff_block, (diag_blocks, couplings, masked_rows)).astype(jnp.bfloat16)
    block = jnp.einsum("dc,edk->eck", prolong_f, stiff.astype(jnp.float32))
    element = jnp.arange(ELEMS, dtype=jnp.int32)
    group_key = ((element // E_DEV) // N_GY * SUBS + subset).astype(jnp.int32)
    groups = N_GX * SUBS
    coarse_rhs = jax.ops.segment_sum(restricted, group_key, groups)
    coarse_matrix = jax.ops.segment_sum(block, group_key, groups)
    members = jax.ops.segment_sum(jnp.ones((ELEMS,), jnp.float32), group_key, groups)
    theta = 0.5 / jnp.maximum(members, 1.0)
    coarse = jnp.zeros_like(coarse_rhs)
    for sweep in range(CITER):
        applied = jnp.einsum("sck,skr->scr", coarse_matrix, coarse, precision=lax.Precision.HIGHEST)
        coarse = coarse + theta[:, None, None] * (coarse_rhs - applied)
    coarse_b = coarse.astype(jnp.bfloat16)
    picked = coarse_b[group_key]
    state = first + jnp.einsum("dc,ecr->edr", prolong_f, picked.astype(jnp.float32))
    for sweep in range(2):
        resid = residual_of(state, rhs, diag_blocks, couplings, neighbours, live)
        state = state + 0.7 * blockwise(batch_diag, (inverse_blocks, resid.astype(jnp.bfloat16)))
    return state
```

```python
import functools

import jax
import jax.numpy as jnp
from jax import lax
from jax.experimental import pallas as pl
from jax.experimental.pallas import tpu as pltpu
from jax.sharding import PartitionSpec as P

BF = jnp.bfloat16
F32 = jnp.float32
DOF = 384
FDOF = 96
CDOF = 48
LANES = 128
E_DEV = 8
CITER = 4
KLOC = 768
KREM = 256
relax_fine = 0.7
relax_coarse = 0.5


def mm(a, b):
    return jnp.dot(a, b, preferred_element_type=F32)


def x_trace(ref, node):
    return ref[pl.ds(node, FDOF, stride=4), :]


def y_trace(value, node):
    tiles = value.reshape(12, 4, 8, LANES)
    upper = lax.broadcasted_iota(jnp.int32, (12, 8, LANES), 1) < 4
    if node == 0:
        low, high = tiles[:, 0], pltpu.roll(tiles[:, 2], 4, axis=1)
    else:
        low, high = pltpu.roll(tiles[:, 1], 4, axis=1), tiles[:, 3]
    return jnp.where(upper, low, high).reshape(FDOF, LANES)


def z_trace(value, node):
    return value.reshape(6, 4, 16, LANES)[:, node].reshape(FDOF, LANES)


def kernel(
    n_gx, n_gy,
    rhs_h, diag_h, inv_h, coup_h, prol_h, face_s, sub_s,
    out_h,
    rhs_v, inv_v, coup_v, prol_v, w_loc, w_rem, stack, x_v, r_v,
    prol_f, prol_b, prol_t, prol_face, send_b, near,
    rest_v, block_v, part_m, part_r, got_m, got_r, y_all,
    load_sem, coup_sem, out_sem, halo_send, halo_recv, coarse_send, coarse_recv,
):
    gx = lax.axis_index("gx")
    gy = lax.axis_index("gy")
    west, east = lax.rem(gx + n_gx - 1, n_gx), lax.rem(gx + 1, n_gx)
    south, north = lax.rem(gy + n_gy - 1, n_gy), lax.rem(gy + 1, n_gy)
    steps = sorted(range(1, n_gy), key=lambda t: -min(t, n_gy - t))

    barrier = pltpu.get_barrier_semaphore()
    for other in (west, east):
        pl.semaphore_signal(barrier, inc=1, device_id={"gx": other}, device_id_type=pl.DeviceIdType.MESH)
    for t in steps:
        pl.semaphore_signal(
            barrier, inc=1, device_id={"gy": lax.rem(gy + t, n_gy)}, device_id_type=pl.DeviceIdType.MESH
        )

    def load(kind, e):
        if kind == 0:
            return pltpu.make_async_copy(rhs_h.at[e], rhs_v.at[e], load_sem.at[0, e])
        if kind == 1:
            return pltpu.make_async_copy(inv_h.at[e], inv_v.at[e], load_sem.at[1, e])
        return pltpu.make_async_copy(diag_h.at[e], w_loc.at[e, :, pl.ds(0, DOF)], load_sem.at[2, e])

    def load_faces(e):
        k = e // 4
        return (
            pltpu.make_async_copy(coup_h.at[e, pl.ds(0, 4)], coup_v.at[e, pl.ds(0, 4)], coup_sem.at[0, e]),
            pltpu.make_async_copy(coup_h.at[e, 5 - k], coup_v.at[e, 5 - k], coup_sem.at[1, e]),
        )

    prol_load = pltpu.make_async_copy(prol_h, prol_v, out_sem.at[E_DEV])
    for e in range(E_DEV):
        load(0, e).start()
        load(1, e).start()
    prol_load.start()
    for e in range(E_DEV):
        load(2, e).start()
        for copy in load_faces(e):
            copy.start()

    def halo(h, e):
        i, j = e % 2, e // 2 % 2
        x_to, y_to = (west, east)[i], (south, north)[j]
        x_pair, y_pair = e + 1 - 2 * i, e + 2 - 4 * j
        return (
            pltpu.make_async_remote_copy(
                src_ref=send_b.at[h, e, 0],
                dst_ref=near.at[h, x_pair, pl.ds(0, FDOF)],
                send_sem=halo_send.at[h, e, 0],
                recv_sem=halo_recv.at[h, x_pair, 0],
                device_id={"gx": x_to},
                device_id_type=pl.DeviceIdType.MESH,
            ),
            pltpu.make_async_remote_copy(
                src_ref=send_b.at[h, e, 1],
                dst_ref=near.at[h, y_pair, pl.ds(FDOF, FDOF)],
                send_sem=halo_send.at[h, e, 1],
                recv_sem=halo_recv.at[h, y_pair, 1],
                device_id={"gy": y_to},
                device_id_type=pl.DeviceIdType.MESH,
            ),
        )

    def halo_arrived(h, e):
        for face in range(2):
            pltpu.make_async_remote_copy(
                src_ref=send_b.at[h, e, face],
                dst_ref=near.at[h, e, pl.ds(face * FDOF, FDOF)],
                send_sem=halo_send.at[h, e, face],
                recv_sem=halo_recv.at[h, e, face],
                device_id={"gx": gx},
                device_id_type=pl.DeviceIdType.MESH,
            ).wait_recv()

    def publish(h, e, value):
        i, j, k = e % 2, e // 2 % 2, e // 4
        x_v[e] = value
        stack[e, pl.ds(0, DOF), :] = value.astype(BF)
        send_b[h, e, 0] = x_trace(x_v.at[e], 3 * i).astype(BF)
        send_b[h, e, 1] = y_trace(value, 3 * j).astype(BF)
        for copy in halo(h, e):
            copy.start()
        stack[e + 4 - 8 * k, pl.ds(384, FDOF), :] = z_trace(value, 3 - 3 * k).astype(BF)
        stack[e + 1 - 2 * i, pl.ds(512, FDOF), :] = x_trace(x_v.at[e], 3 - 3 * i).astype(BF)
        stack[e + 2 - 4 * j, pl.ds(608, FDOF), :] = y_trace(value, 3 - 3 * j).astype(BF)

    for e in range(E_DEV):
        stack[e, pl.ds(480, 32), :] = jnp.zeros((32, LANES), BF)
        stack[e, pl.ds(704, 64), :] = jnp.zeros((64, LANES), BF)

    started = False
    for e in range(E_DEV):
        load(0, e).wait()
        load(1, e).wait()
        first = relax_fine * mm(inv_v[e], rhs_v[e])
        if not started:
            pl.semaphore_wait(barrier, n_gy + 1)
            started = True
        publish(0, e, first)

    prol_load.wait()
    prol_f[...] = jnp.zeros((DOF, LANES), F32)
    prol_f[:, pl.ds(0, CDOF)] = prol_v[...].astype(F32)
    prol_full = prol_f[...]
    prol_b[...] = prol_full.astype(BF)
    prol_t[...] = jnp.transpose(prol_full)[:CDOF].astype(BF)
    for node in range(2):
        prol_face[0 + 1 - node] = x_trace(prol_f, 3 * node).astype(BF)
        prol_face[2 + 1 - node] = y_trace(prol_full, 3 * node).astype(BF)
        prol_face[4 + 1 - node] = z_trace(prol_full, 3 * node).astype(BF)

    zeros_32 = jnp.zeros((32, LANES), BF)
    zeros_64 = jnp.zeros((64, LANES), BF)
    one_at = (lax.broadcasted_iota(jnp.int32, (CDOF, LANES), 1) == CDOF).astype(F32)

    for e in range(E_DEV):
        i, j, k = e % 2, e // 2 % 2, e // 4
        load(2, e).wait()
        for copy in load_faces(e):
            copy.wait()

        def face(f):
            live = (face_s[e, f] > 0).astype(F32).astype(BF)
            return coup_v[e, f] * live

        pad_32, pad_64 = jnp.zeros((DOF, 32), BF), jnp.zeros((DOF, 64), BF)
        w_loc[e, :, pl.ds(384, 128)] = jnp.concatenate([face(5 - k), pad_32], axis=1)
        w_loc[e, :, pl.ds(512, 256)] = jnp.concatenate([face(1 - i), face(3 - j), pad_64], axis=1)
        w_rem[e] = jnp.concatenate([face(i), face(2 + j), pad_64], axis=1)
        prol_stack = jnp.concatenate(
            [prol_b[...], prol_face[5 - k], zeros_32, prol_face[1 - i], prol_face[3 - j], zeros_64], axis=0
        )
        both = mm(w_loc[e], jnp.concatenate([stack[e], prol_stack], axis=1))
        r_v[e] = rhs_v[e].astype(F32) - both[:, :LANES]
        outer = mm(w_rem[e], jnp.concatenate([prol_face[i], prol_face[2 + j], zeros_64], axis=0))
        stiff = (both[:, LANES:] + outer).astype(BF)
        block_v[e] = mm(prol_t[...], stiff) + one_at

    def spread(part, source):
        for s in range(n_gy):
            total = jnp.zeros((CDOF, LANES), F32)
            for e in range(E_DEV):
                total = total + (sub_s[e] == s).astype(F32) * source[e]
            part[s] = total.astype(BF)

    def coarse_copy(c, t, src, dst):
        return pltpu.make_async_remote_copy(
            src_ref=src,
            dst_ref=dst,
            send_sem=coarse_send.at[c, t],
            recv_sem=coarse_recv.at[c, t],
            device_id={"gy": lax.rem(gy + t, n_gy)},
            device_id_type=pl.DeviceIdType.MESH,
        )

    def scatter(c, part, got):
        return [coarse_copy(c, t, part.at[lax.rem(gy + t, n_gy)], got.at[t]) for t in steps]

    def gathered_sum(c, part, got):
        for copy in scatter(c, part, got):
            copy.wait_recv()
        total = part[gy].astype(F32)
        for t in range(1, n_gy):
            total = total + got[t].astype(F32)
        return total

    spread(part_m, block_v)
    for copy in scatter(0, part_m, got_m):
        copy.start()

    def residual(h, e):
        halo_arrived(h, e)
        return r_v[e] - mm(w_rem[e], jnp.concatenate([near[h, e], zeros_64], axis=0))

    for e in range(E_DEV):
        rest_v[e] = mm(prol_t[...], residual(0, e).astype(BF))
    spread(part_r, rest_v)
    for copy in scatter(1, part_r, got_r):
        copy.start()

    matrix_sum = gathered_sum(0, part_m, got_m)
    matrix = matrix_sum[:, :CDOF]
    theta = relax_coarse / jnp.maximum(matrix_sum[:, CDOF:CDOF + 1], 1.0)
    coarse_rhs = gathered_sum(1, part_r, got_r)
    coarse = theta * coarse_rhs
    for sweep in range(CITER - 1):
        applied = jnp.dot(matrix, coarse, precision=lax.Precision.HIGHEST, preferred_element_type=F32)
        coarse = coarse + theta * (coarse_rhs - applied)
    y_all[gy] = coarse.astype(BF)
    y_copies = [coarse_copy(2, t, y_all.at[gy], y_all.at[gy]) for t in steps]
    for copy in y_copies:
        copy.start()
    for t in steps:
        came = lax.rem(gy + n_gy - t, n_gy)
        coarse_copy(2, t, y_all.at[came], y_all.at[came]).wait_recv()

    zeros_80 = jnp.zeros((LANES - CDOF, LANES), BF)
    for e in range(E_DEV):
        picked = jnp.concatenate([y_all[sub_s[e]], zeros_80], axis=0)
        publish(1, e, x_v[e] + mm(prol_b[...], picked))

    for sweep in range(2):
        h = sweep + 1
        for e in range(E_DEV):
            r_v[e] = rhs_v[e].astype(F32) - mm(w_loc[e], stack[e])
        for e in range(E_DEV):
            state = x_v[e] + relax_fine * mm(inv_v[e], residual(h, e).astype(BF))
            if sweep == 0:
                publish(2, e, state)
            else:
                x_v[e] = state
                pltpu.make_async_copy(x_v.at[e], out_h.at[e], out_sem.at[e]).start()

    for e in range(E_DEV):
        for h in range(3):
            for copy in halo(h, e):
                copy.wait_send()
        pltpu.make_async_copy(x_v.at[e], out_h.at[e], out_sem.at[e]).wait()
    for copy in scatter(0, part_m, got_m) + scatter(1, part_r, got_r) + y_copies:
        copy.wait_send()


def on_device(n_gx, n_gy, rhs, diag_blocks, inverse_blocks, couplings, prolong, face_source, subset):
    any_space = pl.BlockSpec(memory_space=pl.ANY)
    smem = pl.BlockSpec(memory_space=pltpu.SMEM)
    dma = pltpu.SemaphoreType.DMA
    return pl.pallas_call(
        functools.partial(kernel, n_gx, n_gy),
        out_shape=jax.ShapeDtypeStruct((E_DEV, DOF, LANES), F32),
        in_specs=[any_space] * 5 + [smem, smem],
        out_specs=any_space,
        scratch_shapes=[
            pltpu.VMEM((E_DEV, DOF, LANES), BF),
            pltpu.VMEM((E_DEV, DOF, DOF), BF),
            pltpu.VMEM((E_DEV, 6, DOF, FDOF), BF),
            pltpu.VMEM((DOF, CDOF), BF),
            pltpu.VMEM((E_DEV, DOF, KLOC), BF),
            pltpu.VMEM((E_DEV, DOF, KREM), BF),
            pltpu.VMEM((E_DEV, KLOC, LANES), BF),
            pltpu.VMEM((E_DEV, DOF, LANES), F32),
            pltpu.VMEM((E_DEV, DOF, LANES), F32),
            pltpu.VMEM((DOF, LANES), F32),
            pltpu.VMEM((DOF, LANES), BF),
            pltpu.VMEM((CDOF, DOF), BF),
            pltpu.VMEM((6, FDOF, LANES), BF),
            pltpu.VMEM((3, E_DEV, 2, FDOF, LANES), BF),
            pltpu.VMEM((3, E_DEV, 2 * FDOF, LANES), BF),
            pltpu.VMEM((E_DEV, CDOF, LANES), F32),
            pltpu.VMEM((E_DEV, CDOF, LANES), F32),
            pltpu.VMEM((n_gy, CDOF, LANES), BF),
            pltpu.VMEM((n_gy, CDOF, LANES), BF),
            pltpu.VMEM((n_gy, CDOF, LANES), BF),
            pltpu.VMEM((n_gy, CDOF, LANES), BF),
            pltpu.VMEM((n_gy, CDOF, LANES), BF),
            dma((3, E_DEV)),
            dma((2, E_DEV)),
            dma((E_DEV + 1,)),
            dma((3, E_DEV, 2)),
            dma((3, E_DEV, 2)),
            dma((3, n_gy)),
            dma((3, n_gy)),
        ],
        compiler_params=pltpu.CompilerParams(
            collective_id=0, has_side_effects=True, vmem_limit_bytes=60 * 1024 * 1024
        ),
    )(rhs, diag_blocks, inverse_blocks, couplings, prolong, face_source, subset)


def solution(mesh):
    return jax.shard_map(
        functools.partial(on_device, mesh.shape["gx"], mesh.shape["gy"]),
        mesh=mesh,
        in_specs=(
            P(("gx", "gy"), None, None),
            P(("gx", "gy"), None, None),
            P(("gx", "gy"), None, None),
            P(("gx", "gy"), None, None, None),
            P(),
            P(("gx", "gy"), None),
            P(("gx", "gy")),
        ),
        out_specs=P(("gx", "gy"), None, None),
        check_vma=False,
    )
```

```python
import functools

import jax
import jax.numpy as jnp
from jax import lax
from jax.experimental import pallas as pl
from jax.experimental.pallas import tpu as pltpu
from jax.sharding import PartitionSpec as P

BF = jnp.bfloat16
F32 = jnp.float32
DOF = 384
FDOF = 96
CDOF = 48
LANES = 128
E_DEV = 8
CITER = 4
KLOC = 768
KREM = 256
relax_fine = 0.7
relax_coarse = 0.5


def mm(a, b):
    return jnp.dot(a, b, preferred_element_type=F32)


WHOLE = (pl.ds(0, DOF),)
HALVES = (pl.ds(0, DOF // 2), pl.ds(DOF // 2, DOF // 2))


def x_trace(ref, node):
    return ref[pl.ds(node, FDOF, stride=4), :]


def y_trace(value, node):
    tiles = value.reshape(12, 4, 8, LANES)
    upper = lax.broadcasted_iota(jnp.int32, (12, 8, LANES), 1) < 4
    if node == 0:
        low, high = tiles[:, 0], pltpu.roll(tiles[:, 2], 4, axis=1)
    else:
        low, high = pltpu.roll(tiles[:, 1], 4, axis=1), tiles[:, 3]
    return jnp.where(upper, low, high).reshape(FDOF, LANES)


def z_trace(value, node):
    return value.reshape(6, 4, 16, LANES)[:, node].reshape(FDOF, LANES)


def kernel(
    n_gx, n_gy,
    rhs_h, diag_h, inv_h, coup_h, prol_h, face_s, sub_s,
    out_v,
    rhs_v, inv_v, face_t, w_all, stack, x_v, r_v, rb_v,
    prol_f, prol_b, prol_t, prol_face, send_b, near,
    rest_v, block_v, stiff_v, part_m, part_r, pair_m, pair_r, chip_m, chip_r, got_m, got_r, y_all, share_s,
    inv_sem, load_sem, halo_send, halo_recv, pair_send, pair_recv, ring_send, ring_recv, y_recv,
):
    gx = lax.axis_index("gx")
    gy = lax.axis_index("gy")
    west, east = lax.rem(gx + n_gx - 1, n_gx), lax.rem(gx + 1, n_gx)
    south, north = lax.rem(gy + n_gy - 1, n_gy), lax.rem(gy + 1, n_gy)
    core, z, n_z = lax.rem(gy, 2), gy // 2, n_gy // 2
    sibling = gy + 1 - 2 * core
    hops = sorted(range(1, n_z), key=lambda d: -min(d, n_z - d))
    row_partners = sorted({1, n_gy - 1} | {2 * d for d in hops})
    half = E_DEV // 2

    inv_loads = [pltpu.make_async_copy(inv_h.at[e], inv_v.at[e], inv_sem.at[e]) for e in range(E_DEV)]
    rhs_loads = [
        pltpu.make_async_copy(rhs_h.at[pl.ds(g * half, half)], rhs_v.at[pl.ds(g * half, half)], load_sem.at[g])
        for g in range(2)
    ]
    late_loads = [pltpu.make_async_copy(prol_h, prol_t, load_sem.at[2])]
    for g in range(2):
        part = pl.ds(g * half, half)
        late_loads += [
            pltpu.make_async_copy(coup_h.at[part, pl.ds(0, 4)], face_t.at[part, pl.ds(0, 4)], load_sem.at[3 + g]),
            pltpu.make_async_copy(coup_h.at[part, 5 - g], face_t.at[part, 4], load_sem.at[5 + g]),
            pltpu.make_async_copy(diag_h.at[part], w_all.at[part, :, pl.ds(0, DOF)], load_sem.at[7 + g]),
        ]
    inv_loads[0].start()
    rhs_loads[0].start()
    for copy in inv_loads[1:]:
        copy.start()
    rhs_loads[1].start()

    barrier = pltpu.get_barrier_semaphore()
    for other in (west, east):
        pl.semaphore_signal(barrier, inc=1, device_id={"gx": other}, device_id_type=pl.DeviceIdType.MESH)
    for t in row_partners:
        pl.semaphore_signal(
            barrier, inc=1, device_id={"gy": lax.rem(gy + t, n_gy)}, device_id_type=pl.DeviceIdType.MESH
        )
    for copy in late_loads:
        copy.start()

    def halo(h, e):
        i, j = e % 2, e // 2 % 2
        x_to, y_to = (west, east)[i], (south, north)[j]
        x_pair, y_pair = e + 1 - 2 * i, e + 2 - 4 * j
        return (
            pltpu.make_async_remote_copy(
                src_ref=send_b.at[h, e, 0],
                dst_ref=near.at[h, x_pair, pl.ds(0, FDOF)],
                send_sem=halo_send.at[h],
                recv_sem=halo_recv.at[h, x_pair],
                device_id={"gx": x_to},
                device_id_type=pl.DeviceIdType.MESH,
            ),
            pltpu.make_async_remote_copy(
                src_ref=send_b.at[h, e, 1],
                dst_ref=near.at[h, y_pair, pl.ds(FDOF, FDOF)],
                send_sem=halo_send.at[h],
                recv_sem=halo_recv.at[h, y_pair],
                device_id={"gy": y_to},
                device_id_type=pl.DeviceIdType.MESH,
            ),
        )

    def halo_arrived(h, e):
        pltpu.make_async_copy(near.at[h, e], near.at[h, e], halo_recv.at[h, e]).wait()

    def publish(h, e):
        i, j, k = e % 2, e // 2 % 2, e // 4
        ref = x_v.at[e]
        value = ref[...]
        send_b[h, e, 0] = x_trace(ref, 3 * i).astype(BF)
        send_b[h, e, 1] = y_trace(value, 3 * j).astype(BF)
        stack[e, pl.ds(0, DOF), :] = value.astype(BF)
        stack[e + 4 - 8 * k, pl.ds(384, FDOF), :] = z_trace(value, 3 - 3 * k).astype(BF)
        stack[e + 1 - 2 * i, pl.ds(512, FDOF), :] = x_trace(ref, 3 - 3 * i).astype(BF)
        stack[e + 2 - 4 * j, pl.ds(608, FDOF), :] = y_trace(value, 3 - 3 * j).astype(BF)

    def launch(h, e):
        for copy in halo(h, e):
            copy.start()

    for e in range(E_DEV):
        stack[e, pl.ds(480, 32), :] = jnp.zeros((32, LANES), BF)
        stack[e, pl.ds(704, 64), :] = jnp.zeros((64, LANES), BF)
    for s in range(n_gy):
        for e in range(E_DEV):
            share_s[s, e] = (sub_s[e] == s).astype(F32)

    for t in range(E_DEV + 1):
        if t < E_DEV:
            inv_loads[t].wait()
            if t % half == 0:
                rhs_loads[t // half].wait()
        if t >= 1:
            publish(0, t - 1)
        if t < E_DEV:
            for rows in HALVES:
                x_v[t, rows, :] = relax_fine * mm(inv_v[t, rows, :], rhs_v[t])
        if t == 1:
            pl.semaphore_wait(barrier, len(row_partners) + 2)
        if t >= 1:
            launch(0, t - 1)

    for copy in late_loads:
        copy.wait()
    prol_pad = jnp.concatenate([prol_t[...].astype(F32), jnp.zeros((LANES - CDOF, DOF), F32)], axis=0)
    prol_full = jnp.transpose(prol_pad)
    prol_f[...] = prol_full
    prol_b[...] = prol_full.astype(BF)
    for node in range(2):
        prol_face[0 + 1 - node] = x_trace(prol_f, 3 * node).astype(BF)
        prol_face[2 + 1 - node] = y_trace(prol_full, 3 * node).astype(BF)
        prol_face[4 + 1 - node] = z_trace(prol_full, 3 * node).astype(BF)

    zeros_32 = jnp.zeros((32, LANES), BF)
    zeros_64 = jnp.zeros((64, LANES), BF)
    one_at = (lax.broadcasted_iota(jnp.int32, (CDOF // 2, LANES), 1) == 2 * CDOF).astype(F32)

    def pack(e):
        i, j, k = e % 2, e // 2 % 2, e // 4

        def face(f):
            live = (face_s[e, f] > 0).astype(F32).astype(BF)
            return face_t[e, min(f, 4)] * live

        pad_32, pad_64 = jnp.zeros((32, DOF), BF), jnp.zeros((64, DOF), BF)
        z_part = jnp.concatenate([face(5 - k), pad_32], axis=0)
        near_part = jnp.concatenate([face(1 - i), face(3 - j), pad_64], axis=0)
        far_part = jnp.concatenate([face(i), face(2 + j), pad_64], axis=0)
        w_all[e, :, pl.ds(DOF, 128)] = jnp.transpose(z_part)
        w_all[e, :, pl.ds(512, 256)] = jnp.transpose(near_part)
        w_all[e, :, pl.ds(KLOC, KREM)] = jnp.transpose(far_part)

    def local_both(e):
        i, j, k = e % 2, e // 2 % 2, e // 4
        prol_stack = jnp.concatenate(
            [
                prol_b[...], prol_face[5 - k], zeros_32, prol_face[1 - i], prol_face[3 - j], zeros_64,
                prol_face[i], prol_face[2 + j], zeros_64,
            ],
            axis=0,
        )
        state = jnp.concatenate([stack[e], jnp.zeros((KREM, LANES), BF)], axis=0)
        for rows in HALVES:
            both = mm(w_all[e, rows, :], jnp.concatenate([state, prol_stack], axis=1))
            r_v[e, rows, :] = rhs_v[e, rows, :].astype(F32) - both[:, :LANES]
            stiff_v[e, rows, :] = both[:, LANES:].astype(BF)

    for t in range(E_DEV + 2):
        if t < E_DEV:
            pack(t)
        if 1 <= t <= E_DEV:
            local_both(t - 1)
        if t >= 2:
            block = mm(prol_t[...], stiff_v[t - 2])
            block_v[t - 2] = block[:CDOF // 2] + pltpu.roll(block[CDOF // 2:], CDOF, axis=1) + one_at

    def spread(part, source, size):
        for c in range(source.shape[1] // size):
            rows = pl.ds(c * size, size)
            pieces = [source[e, rows, :] for e in range(E_DEV)]
            for s in range(n_gy):
                total = share_s[s, 0] * pieces[0]
                for e in range(1, E_DEV):
                    total = total + share_s[s, e] * pieces[e]
                part[s % 2, s // 2, rows, :] = total.astype(BF)

    def remote(to, src, dst, send_sem, recv_sem):
        return pltpu.make_async_remote_copy(
            src_ref=src,
            dst_ref=dst,
            send_sem=send_sem,
            recv_sem=recv_sem,
            device_id={"gy": to},
            device_id_type=pl.DeviceIdType.MESH,
        )

    def same_core(d):
        return 2 * lax.rem(z + d, n_z) + core

    def pair_copy(c, part, pair):
        return remote(sibling, part.at[1 - core], pair, pair_send.at[c], pair_recv.at[c])

    def scatter(c, part, pair, chip, got):
        pair_copy(c, part, pair).wait_recv()
        for at in range(n_z):
            chip[at] = (part[core, at].astype(F32) + pair[at].astype(F32)).astype(BF)
        for d in hops:
            remote(
                same_core(d), chip.at[lax.rem(z + d, n_z)], got.at[d - 1], ring_send.at[c], ring_recv.at[c]
            ).start()

    def all_of(got, sem):
        return pltpu.make_async_copy(got, got, sem)

    def gathered_sum(c, part, pair, got):
        total = part[core, z].astype(F32) + pair[z].astype(F32)
        if n_z > 1:
            all_of(got, ring_recv.at[c]).wait()
            for d in hops:
                total = total + got[d - 1].astype(F32)
        return total

    spread(part_m, block_v, CDOF // 2)
    pair_copy(0, part_m, pair_m).start()

    def residual(h, e):
        far = jnp.concatenate([near[h, e], zeros_64], axis=0)
        for rows in HALVES:
            rb_v[e, rows, :] = (r_v[e, rows, :] - mm(w_all[e, rows, pl.ds(KLOC, KREM)], far)).astype(BF)

    for t in range(E_DEV + 1):
        if t == 2:
            scatter(0, part_m, pair_m, chip_m, got_m)
        if t < E_DEV:
            halo_arrived(0, t)
            residual(0, t)
        if t >= 1:
            rest_v[t - 1] = mm(prol_t[...], rb_v[t - 1])
    spread(part_r, rest_v, 16)
    pair_copy(1, part_r, pair_r).start()
    scatter(1, part_r, pair_r, chip_r, got_r)

    matrix_sum = gathered_sum(0, part_m, pair_m, got_m)
    matrix = jnp.concatenate(
        [matrix_sum[:, :CDOF], pltpu.roll(matrix_sum, LANES - CDOF, axis=1)[:, :CDOF]], axis=0
    )
    theta = relax_coarse / jnp.maximum(matrix_sum[:1, 2 * CDOF:2 * CDOF + 1], 1.0)
    coarse_rhs = gathered_sum(1, part_r, pair_r, got_r)
    coarse = theta * coarse_rhs
    for sweep in range(CITER - 1):
        applied = jnp.dot(matrix, coarse, precision=lax.Precision.HIGHEST, preferred_element_type=F32)
        coarse = coarse + theta * (coarse_rhs - applied)
    y_all[gy] = coarse.astype(BF)
    for d in hops:
        remote(same_core(d), y_all.at[gy], y_all.at[gy], ring_send.at[2], y_recv.at[d]).start()
    remote(sibling, y_all.at[gy], y_all.at[gy], pair_send.at[2], pair_recv.at[2]).start()
    pltpu.make_async_copy(send_b.at[0], send_b.at[0], halo_send.at[0]).wait()
    for c, part in ((0, part_m), (1, part_r)):
        all_of(part.at[0], pair_send.at[c]).wait()
    if n_z > 1:
        all_of(got_m, ring_send.at[0]).wait()
        all_of(got_r, ring_send.at[1]).wait()
    for d in reversed(hops):
        came = same_core(n_z - d)
        remote(sibling, y_all.at[came], y_all.at[came], pair_send.at[2], y_recv.at[d]).wait_recv()
        remote(sibling, y_all.at[came], y_all.at[came], pair_send.at[2], pair_recv.at[2]).start()
    all_of(part_r.at[0], pair_recv.at[2]).wait()

    zeros_80 = jnp.zeros((LANES - CDOF, LANES), BF)
    for t in range(E_DEV + 1):
        if t >= 1:
            publish(1, t - 1)
        if t < E_DEV:
            picked = jnp.concatenate([y_all[sub_s[t]], zeros_80], axis=0)
            for rows in HALVES:
                x_v[t, rows, :] = x_v[t, rows, :] + mm(prol_b[rows, :], picked)
        if t >= 1:
            launch(1, t - 1)

    for h in (1, 2):
        for e in range(E_DEV):
            for rows in WHOLE:
                r_v[e, rows, :] = rhs_v[e, rows, :].astype(F32) - mm(w_all[e, rows, pl.ds(0, KLOC)], stack[e])
        if h == 2:
            pltpu.make_async_copy(send_b.at[1], send_b.at[1], halo_send.at[1]).wait()
            all_of(part_r.at[0], pair_send.at[2]).wait()
            if n_z > 1:
                all_of(got_r, ring_send.at[2]).wait()
        for t in range(E_DEV + 2):
            if t < E_DEV:
                halo_arrived(h, t)
            if t >= 2 and h == 1:
                publish(2, t - 2)
            if t < E_DEV:
                residual(h, t)
            if 1 <= t <= E_DEV:
                target = x_v if h == 1 else out_v
                for rows in HALVES:
                    target[t - 1, rows, :] = x_v[t - 1, rows, :] + relax_fine * mm(inv_v[t - 1, rows, :], rb_v[t - 1])
            if t >= 2 and h == 1:
                launch(2, t - 2)
    pltpu.make_async_copy(send_b.at[2], send_b.at[2], halo_send.at[2]).wait()


def on_device(n_gx, n_gy, rhs, diag_blocks, inverse_blocks, couplings, prolong, face_source, subset):
    any_space = pl.BlockSpec(memory_space=pl.ANY)
    smem = pl.BlockSpec(memory_space=pltpu.SMEM)
    dma = pltpu.SemaphoreType.DMA
    n_z = n_gy // 2
    return pl.pallas_call(
        functools.partial(kernel, n_gx, n_gy),
        out_shape=pltpu.VMEM((E_DEV, DOF, LANES), F32),
        in_specs=[any_space] * 5 + [smem, smem],
        out_specs=pl.BlockSpec(memory_space=pltpu.VMEM),
        scratch_shapes=[
            pltpu.VMEM((E_DEV, DOF, LANES), BF),
            pltpu.VMEM((E_DEV, DOF, DOF), BF),
            pltpu.VMEM((E_DEV, 5, FDOF, DOF), BF),
            pltpu.VMEM((E_DEV, DOF, KLOC + KREM), BF),
            pltpu.VMEM((E_DEV, KLOC, LANES), BF),
            pltpu.VMEM((E_DEV, DOF, LANES), F32),
            pltpu.VMEM((E_DEV, DOF, LANES), F32),
            pltpu.VMEM((E_DEV, DOF, LANES), BF),
            pltpu.VMEM((DOF, LANES), F32),
            pltpu.VMEM((DOF, LANES), BF),
            pltpu.VMEM((CDOF, DOF), BF),
            pltpu.VMEM((6, FDOF, LANES), BF),
            pltpu.VMEM((3, E_DEV, 2, FDOF, LANES), BF),
            pltpu.VMEM((3, E_DEV, 2 * FDOF, LANES), BF),
            pltpu.VMEM((E_DEV, CDOF, LANES), F32),
            pltpu.VMEM((E_DEV, CDOF // 2, LANES), F32),
            pltpu.VMEM((E_DEV, DOF, LANES), BF),
            pltpu.VMEM((2, n_z, CDOF // 2, LANES), BF),
            pltpu.VMEM((2, n_z, CDOF, LANES), BF),
            pltpu.VMEM((n_z, CDOF // 2, LANES), BF),
            pltpu.VMEM((n_z, CDOF, LANES), BF),
            pltpu.VMEM((n_z, CDOF // 2, LANES), BF),
            pltpu.VMEM((n_z, CDOF, LANES), BF),
            pltpu.VMEM((max(n_z - 1, 1), CDOF // 2, LANES), BF),
            pltpu.VMEM((max(n_z - 1, 1), CDOF, LANES), BF),
            pltpu.VMEM((n_gy, CDOF, LANES), BF),
            pltpu.SMEM((n_gy, E_DEV), F32),
            dma((E_DEV,)),
            dma((9,)),
            dma((3,)),
            dma((3, E_DEV)),
            dma((3,)),
            dma((3,)),
            dma((3,)),
            dma((2,)),
            dma((n_z,)),
        ],
        compiler_params=pltpu.CompilerParams(
            collective_id=0, has_side_effects=True, vmem_limit_bytes=56 * 1024 * 1024
        ),
    )(rhs, diag_blocks, inverse_blocks, jnp.swapaxes(couplings, 2, 3), prolong.T, face_source, subset)


def solution(mesh):
    return jax.shard_map(
        functools.partial(on_device, mesh.shape["gx"], mesh.shape["gy"]),
        mesh=mesh,
        in_specs=(
            P(("gx", "gy"), None, None),
            P(("gx", "gy"), None, None),
            P(("gx", "gy"), None, None),
            P(("gx", "gy"), None, None, None),
            P(),
            P(("gx", "gy"), None),
            P(("gx", "gy")),
        ),
        out_specs=P(("gx", "gy"), None, None),
        check_vma=False,
    )
```

```python
import functools

import jax
import jax.numpy as jnp
from jax import lax
from jax.experimental import pallas as pl
from jax.experimental.pallas import tpu as pltpu
from jax.sharding import PartitionSpec as P

BF = jnp.bfloat16
F32 = jnp.float32
DOF = 384
FDOF = 96
CDOF = 48
LANES = 128
E_DEV = 8
CITER = 4
KLOC = 768
KREM = 256
relax_fine = 0.7
relax_coarse = 0.5


def mm(a, b):
    return jnp.dot(a, b, preferred_element_type=F32)


WHOLE = (pl.ds(0, DOF),)
HALVES = (pl.ds(0, DOF // 2), pl.ds(DOF // 2, DOF // 2))


def x_trace(ref, node):
    return ref[pl.ds(node, FDOF, stride=4), :]


def y_trace(value, node):
    tiles = value.reshape(12, 4, 8, LANES)
    upper = lax.broadcasted_iota(jnp.int32, (12, 8, LANES), 1) < 4
    if node == 0:
        low, high = tiles[:, 0], pltpu.roll(tiles[:, 2], 4, axis=1)
    else:
        low, high = pltpu.roll(tiles[:, 1], 4, axis=1), tiles[:, 3]
    return jnp.where(upper, low, high).reshape(FDOF, LANES)


def z_trace(value, node):
    return value.reshape(6, 4, 16, LANES)[:, node].reshape(FDOF, LANES)


def kernel(
    n_gx, n_gy,
    rhs_h, diag_h, inv_h, coup_h, prol_h, face_h, sub_h,
    out_v,
    rhs_v, inv_v, face_t, w_all, stack, x_v, r_v, rb_v,
    prol_f, prol_b, prol_t, prol_face, send_b, near,
    rest_v, block_v, stiff_v, part_m, part_r, pair_m, pair_r, chip_m, chip_r, got_m, got_r, y_all, share_s, face_s, sub_s,
    inv_sem, load_sem, halo_send, halo_recv, pair_send, pair_recv, ring_send, ring_recv, y_recv,
):
    gx = lax.axis_index("gx")
    gy = lax.axis_index("gy")
    west, east = lax.rem(gx + n_gx - 1, n_gx), lax.rem(gx + 1, n_gx)
    south, north = lax.rem(gy + n_gy - 1, n_gy), lax.rem(gy + 1, n_gy)
    core, z, n_z = lax.rem(gy, 2), gy // 2, n_gy // 2
    sibling = gy + 1 - 2 * core
    hops = sorted(range(1, n_z), key=lambda d: -min(d, n_z - d))
    row_partners = sorted({1, n_gy - 1} | {2 * d for d in hops}, key=lambda t: -min(t, n_gy - t))
    half = E_DEV // 2

    inv_loads = [pltpu.make_async_copy(inv_h.at[e], inv_v.at[e], inv_sem.at[e]) for e in range(E_DEV)]
    first_part, rest_part = pl.ds(0, 1), pl.ds(1, E_DEV - 1)
    rhs_loads = [
        pltpu.make_async_copy(rhs_h.at[part], rhs_v.at[part], load_sem.at[g])
        for g, part in enumerate((first_part, rest_part))
    ]
    late_loads = [
        pltpu.make_async_copy(prol_h, prol_t, load_sem.at[2]),
        pltpu.make_async_copy(face_h, face_s, load_sem.at[9]),
        pltpu.make_async_copy(sub_h, sub_s, load_sem.at[10]),
    ]
    for g in range(2):
        part = pl.ds(g * half, half)
        late_loads += [
            pltpu.make_async_copy(coup_h.at[part, pl.ds(0, 4)], face_t.at[part, pl.ds(0, 4)], load_sem.at[3 + g]),
            pltpu.make_async_copy(coup_h.at[part, 5 - g], face_t.at[part, 4], load_sem.at[5 + g]),
            pltpu.make_async_copy(diag_h.at[part], w_all.at[part, :, pl.ds(0, DOF)], load_sem.at[7 + g]),
        ]
    barrier = pltpu.get_barrier_semaphore()
    for t in row_partners:
        pl.semaphore_signal(
            barrier, inc=1, device_id={"gy": lax.rem(gy + t, n_gy)}, device_id_type=pl.DeviceIdType.MESH
        )
    for other in (west, east):
        pl.semaphore_signal(barrier, inc=1, device_id={"gx": other}, device_id_type=pl.DeviceIdType.MESH)

    inv_loads[0].start()
    rhs_loads[0].start()
    rhs_loads[1].start()
    for copy in inv_loads[1:]:
        copy.start()

    def halo(h, e):
        i, j = e % 2, e // 2 % 2
        x_to, y_to = (west, east)[i], (south, north)[j]
        x_pair, y_pair = e + 1 - 2 * i, e + 2 - 4 * j
        return (
            pltpu.make_async_remote_copy(
                src_ref=send_b.at[h, e, 0],
                dst_ref=near.at[h, x_pair, pl.ds(0, FDOF)],
                send_sem=halo_send.at[h],
                recv_sem=halo_recv.at[h, x_pair],
                device_id={"gx": x_to},
                device_id_type=pl.DeviceIdType.MESH,
            ),
            pltpu.make_async_remote_copy(
                src_ref=send_b.at[h, e, 1],
                dst_ref=near.at[h, y_pair, pl.ds(FDOF, FDOF)],
                send_sem=halo_send.at[h],
                recv_sem=halo_recv.at[h, y_pair],
                device_id={"gy": y_to},
                device_id_type=pl.DeviceIdType.MESH,
            ),
        )

    def halo_arrived(h, e):
        pltpu.make_async_copy(near.at[h, e], near.at[h, e], halo_recv.at[h, e]).wait()

    def publish(h, e):
        i, j = e % 2, e // 2 % 2
        ref = x_v.at[e]
        value = ref[...]
        send_b[h, e, 0] = x_trace(ref, 3 * i).astype(BF)
        send_b[h, e, 1] = y_trace(value, 3 * j).astype(BF)

    def settle(e):
        i, j, k = e % 2, e // 2 % 2, e // 4
        ref = x_v.at[e]
        value = ref[...]
        stack[e, pl.ds(0, DOF), :] = value.astype(BF)
        stack[e + 4 - 8 * k, pl.ds(384, FDOF), :] = z_trace(value, 3 - 3 * k).astype(BF)
        stack[e + 1 - 2 * i, pl.ds(512, FDOF), :] = x_trace(ref, 3 - 3 * i).astype(BF)
        stack[e + 2 - 4 * j, pl.ds(608, FDOF), :] = y_trace(value, 3 - 3 * j).astype(BF)

    def launch(h, e):
        for copy in halo(h, e):
            copy.start()

    for e in range(E_DEV):
        stack[e, pl.ds(480, 32), :] = jnp.zeros((32, LANES), BF)
        stack[e, pl.ds(704, 64), :] = jnp.zeros((64, LANES), BF)

    for t in range(E_DEV + 1):
        if t < E_DEV:
            inv_loads[t].wait()
            if t < 2:
                rhs_loads[t].wait()
        if t >= 1:
            publish(0, t - 1)
        if t < E_DEV:
            for rows in HALVES:
                x_v[t, rows, :] = relax_fine * mm(inv_v[t, rows, :], rhs_v[t])
        if t == 3:
            for copy in late_loads:
                copy.start()
        if t == 3:
            pl.semaphore_wait(barrier, len(row_partners) + 2)
            for e in range(3):
                launch(0, e)
        if t > 3:
            launch(0, t - 1)

    for e in range(E_DEV):
        settle(e)
    for copy in late_loads:
        copy.wait()
    for s in range(n_gy):
        for e in range(E_DEV):
            share_s[s, e] = (sub_s[e] == s).astype(F32)
    prol_pad = jnp.concatenate([prol_t[...].astype(F32), jnp.zeros((LANES - CDOF, DOF), F32)], axis=0)
    prol_full = jnp.transpose(prol_pad)
    prol_f[...] = prol_full
    prol_b[...] = prol_full.astype(BF)
    for node in range(2):
        prol_face[0 + 1 - node] = x_trace(prol_f, 3 * node).astype(BF)
        prol_face[2 + 1 - node] = y_trace(prol_full, 3 * node).astype(BF)
        prol_face[4 + 1 - node] = z_trace(prol_full, 3 * node).astype(BF)

    zeros_32 = jnp.zeros((32, LANES), BF)
    zeros_64 = jnp.zeros((64, LANES), BF)
    one_at = (lax.broadcasted_iota(jnp.int32, (CDOF // 2, LANES), 1) == 2 * CDOF).astype(F32)

    def pack(e):
        i, j, k = e % 2, e // 2 % 2, e // 4

        def face(f):
            live = (face_s[e, f] > 0).astype(F32).astype(BF)
            return face_t[e, min(f, 4)] * live

        pad_32, pad_64 = jnp.zeros((32, DOF), BF), jnp.zeros((64, DOF), BF)
        z_part = jnp.concatenate([face(5 - k), pad_32], axis=0)
        near_part = jnp.concatenate([face(1 - i), face(3 - j), pad_64], axis=0)
        far_part = jnp.concatenate([face(i), face(2 + j), pad_64], axis=0)
        w_all[e, :, pl.ds(DOF, 128)] = jnp.transpose(z_part)
        w_all[e, :, pl.ds(512, 256)] = jnp.transpose(near_part)
        w_all[e, :, pl.ds(KLOC, KREM)] = jnp.transpose(far_part)

    def local_both(e):
        i, j, k = e % 2, e // 2 % 2, e // 4
        prol_stack = jnp.concatenate(
            [
                prol_b[...], prol_face[5 - k], zeros_32, prol_face[1 - i], prol_face[3 - j], zeros_64,
                prol_face[i], prol_face[2 + j], zeros_64,
            ],
            axis=0,
        )
        state = jnp.concatenate([stack[e], jnp.zeros((KREM, LANES), BF)], axis=0)
        for rows in HALVES:
            both = mm(w_all[e, rows, :], jnp.concatenate([state, prol_stack], axis=1))
            r_v[e, rows, :] = rhs_v[e, rows, :].astype(F32) - both[:, :LANES]
            stiff_v[e, rows, :] = both[:, LANES:].astype(BF)

    for t in range(E_DEV + 2):
        if t < E_DEV:
            pack(t)
        if 1 <= t <= E_DEV:
            local_both(t - 1)
        if t >= 2:
            block = mm(prol_t[...], stiff_v[t - 2])
            block_v[t - 2] = block[:CDOF // 2] + pltpu.roll(block[CDOF // 2:], CDOF, axis=1) + one_at

    def spread(part, source, size):
        for c in range(source.shape[1] // size):
            rows = pl.ds(c * size, size)
            pieces = [source[e, rows, :] for e in range(E_DEV)]
            for s in range(n_gy):
                total = share_s[s, 0] * pieces[0]
                for e in range(1, E_DEV):
                    total = total + share_s[s, e] * pieces[e]
                part[s % 2, s // 2, rows, :] = total.astype(BF)

    def remote(to, src, dst, send_sem, recv_sem):
        return pltpu.make_async_remote_copy(
            src_ref=src,
            dst_ref=dst,
            send_sem=send_sem,
            recv_sem=recv_sem,
            device_id={"gy": to},
            device_id_type=pl.DeviceIdType.MESH,
        )

    def same_core(d):
        return 2 * lax.rem(z + d, n_z) + core

    def pair_copy(c, part, pair):
        return remote(sibling, part.at[1 - core], pair, pair_send.at[c], pair_recv.at[c])

    def scatter(c, part, pair, chip, got):
        pair_copy(c, part, pair).wait_recv()
        for at in range(n_z):
            chip[at] = (part[core, at].astype(F32) + pair[at].astype(F32)).astype(BF)
        for d in hops:
            remote(
                same_core(d), chip.at[lax.rem(z + d, n_z)], got.at[d - 1], ring_send.at[c], ring_recv.at[c]
            ).start()

    def all_of(got, sem):
        return pltpu.make_async_copy(got, got, sem)

    def gathered_sum(c, part, pair, got):
        total = part[core, z].astype(F32) + pair[z].astype(F32)
        if n_z > 1:
            all_of(got, ring_recv.at[c]).wait()
            for d in hops:
                total = total + got[d - 1].astype(F32)
        return total

    spread(part_m, block_v, CDOF // 2)
    pair_copy(0, part_m, pair_m).start()

    def residual(h, e):
        far = jnp.concatenate([near[h, e], zeros_64], axis=0)
        for rows in HALVES:
            rb_v[e, rows, :] = (r_v[e, rows, :] - mm(w_all[e, rows, pl.ds(KLOC, KREM)], far)).astype(BF)

    for t in range(E_DEV + 1):
        if t < E_DEV:
            halo_arrived(0, t)
            residual(0, t)
        if t >= 1:
            rest_v[t - 1] = mm(prol_t[...], rb_v[t - 1])
    spread(part_r, rest_v, 16)
    pair_copy(1, part_r, pair_r).start()
    scatter(0, part_m, pair_m, chip_m, got_m)
    scatter(1, part_r, pair_r, chip_r, got_r)

    matrix_sum = gathered_sum(0, part_m, pair_m, got_m)
    matrix = jnp.concatenate(
        [matrix_sum[:, :CDOF], pltpu.roll(matrix_sum, LANES - CDOF, axis=1)[:, :CDOF]], axis=0
    )
    matrix_high = matrix.astype(BF)
    matrix_low = (matrix - matrix_high.astype(F32)).astype(BF)
    matrix_parts = jnp.concatenate([matrix_high, matrix_high, matrix_low], axis=1)
    theta = relax_coarse / jnp.maximum(matrix_sum[:1, 2 * CDOF:2 * CDOF + 1], 1.0)
    coarse_rhs = gathered_sum(1, part_r, pair_r, got_r)
    coarse = theta * coarse_rhs
    for sweep in range(CITER - 1):
        high = coarse.astype(BF)
        low = (coarse - high.astype(F32)).astype(BF)
        applied = mm(matrix_parts, jnp.concatenate([high, low, high], axis=0))
        coarse = coarse + theta * (coarse_rhs - applied)
    y_all[gy] = coarse.astype(BF)
    for d in hops:
        remote(same_core(d), y_all.at[gy], y_all.at[gy], ring_send.at[2], y_recv.at[d]).start()
    remote(sibling, y_all.at[gy], y_all.at[gy], pair_send.at[2], pair_recv.at[2]).start()
    pltpu.make_async_copy(send_b.at[0], send_b.at[0], halo_send.at[0]).wait()
    for c, part in ((0, part_m), (1, part_r)):
        all_of(part.at[0], pair_send.at[c]).wait()
    if n_z > 1:
        all_of(got_m, ring_send.at[0]).wait()
        all_of(got_r, ring_send.at[1]).wait()
    for d in reversed(hops):
        came = same_core(n_z - d)
        remote(sibling, y_all.at[came], y_all.at[came], pair_send.at[2], y_recv.at[d]).wait_recv()
        remote(sibling, y_all.at[came], y_all.at[came], pair_send.at[2], pair_recv.at[2]).start()
    all_of(part_r.at[0], pair_recv.at[2]).wait()

    zeros_80 = jnp.zeros((LANES - CDOF, LANES), BF)
    for t in range(E_DEV + 1):
        if t >= 1:
            publish(1, t - 1)
        if t < E_DEV:
            picked = jnp.concatenate([y_all[sub_s[t]], zeros_80], axis=0)
            for rows in HALVES:
                x_v[t, rows, :] = x_v[t, rows, :] + mm(prol_b[rows, :], picked)
        if t >= 1:
            launch(1, t - 1)

    for h in (1, 2):
        for e in range(E_DEV):
            settle(e)
        for e in range(E_DEV):
            for rows in WHOLE:
                r_v[e, rows, :] = rhs_v[e, rows, :].astype(F32) - mm(w_all[e, rows, pl.ds(0, KLOC)], stack[e])
        if h == 2:
            pltpu.make_async_copy(send_b.at[1], send_b.at[1], halo_send.at[1]).wait()
            all_of(part_r.at[0], pair_send.at[2]).wait()
            if n_z > 1:
                all_of(got_r, ring_send.at[2]).wait()
        for t in range(E_DEV + 2):
            if t < E_DEV:
                halo_arrived(h, t)
            if t >= 2 and h == 1:
                publish(2, t - 2)
            if t < E_DEV:
                residual(h, t)
            if 1 <= t <= E_DEV:
                target = x_v if h == 1 else out_v
                for rows in HALVES:
                    target[t - 1, rows, :] = x_v[t - 1, rows, :] + relax_fine * mm(inv_v[t - 1, rows, :], rb_v[t - 1])
            if t >= 2 and h == 1:
                launch(2, t - 2)
    pltpu.make_async_copy(send_b.at[2], send_b.at[2], halo_send.at[2]).wait()


def on_device(n_gx, n_gy, rhs, diag_blocks, inverse_blocks, couplings, prolong, face_source, subset):
    any_space = pl.BlockSpec(memory_space=pl.ANY)
    dma = pltpu.SemaphoreType.DMA
    n_z = n_gy // 2
    return pl.pallas_call(
        functools.partial(kernel, n_gx, n_gy),
        out_shape=pltpu.VMEM((E_DEV, DOF, LANES), F32),
        in_specs=[any_space] * 7,
        out_specs=pl.BlockSpec(memory_space=pltpu.VMEM),
        scratch_shapes=[
            pltpu.VMEM((E_DEV, DOF, LANES), BF),
            pltpu.VMEM((E_DEV, DOF, DOF), BF),
            pltpu.VMEM((E_DEV, 5, FDOF, DOF), BF),
            pltpu.VMEM((E_DEV, DOF, KLOC + KREM), BF),
            pltpu.VMEM((E_DEV, KLOC, LANES), BF),
            pltpu.VMEM((E_DEV, DOF, LANES), F32),
            pltpu.VMEM((E_DEV, DOF, LANES), F32),
            pltpu.VMEM((E_DEV, DOF, LANES), BF),
            pltpu.VMEM((DOF, LANES), F32),
            pltpu.VMEM((DOF, LANES), BF),
            pltpu.VMEM((CDOF, DOF), BF),
            pltpu.VMEM((6, FDOF, LANES), BF),
            pltpu.VMEM((3, E_DEV, 2, FDOF, LANES), BF),
            pltpu.VMEM((3, E_DEV, 2 * FDOF, LANES), BF),
            pltpu.VMEM((E_DEV, CDOF, LANES), F32),
            pltpu.VMEM((E_DEV, CDOF // 2, LANES), F32),
            pltpu.VMEM((E_DEV, DOF, LANES), BF),
            pltpu.VMEM((2, n_z, CDOF // 2, LANES), BF),
            pltpu.VMEM((2, n_z, CDOF, LANES), BF),
            pltpu.VMEM((n_z, CDOF // 2, LANES), BF),
            pltpu.VMEM((n_z, CDOF, LANES), BF),
            pltpu.VMEM((n_z, CDOF // 2, LANES), BF),
            pltpu.VMEM((n_z, CDOF, LANES), BF),
            pltpu.VMEM((max(n_z - 1, 1), CDOF // 2, LANES), BF),
            pltpu.VMEM((max(n_z - 1, 1), CDOF, LANES), BF),
            pltpu.VMEM((n_gy, CDOF, LANES), BF),
            pltpu.SMEM((n_gy, E_DEV), F32),
            pltpu.SMEM((E_DEV, 6), jnp.int32),
            pltpu.SMEM((E_DEV,), jnp.int32),
            dma((E_DEV,)),
            dma((11,)),
            dma((3,)),
            dma((3, E_DEV)),
            dma((3,)),
            dma((3,)),
            dma((3,)),
            dma((2,)),
            dma((n_z,)),
        ],
        compiler_params=pltpu.CompilerParams(
            collective_id=0, has_side_effects=True, vmem_limit_bytes=56 * 1024 * 1024
        ),
    )(rhs, diag_blocks, inverse_blocks, jnp.swapaxes(couplings, 2, 3), prolong.T, face_source, subset)


def solution(mesh):
    return jax.shard_map(
        functools.partial(on_device, mesh.shape["gx"], mesh.shape["gy"]),
        mesh=mesh,
        in_specs=(
            P(("gx", "gy"), None, None),
            P(("gx", "gy"), None, None),
            P(("gx", "gy"), None, None),
            P(("gx", "gy"), None, None, None),
            P(),
            P(("gx", "gy"), None),
            P(("gx", "gy")),
        ),
        out_specs=P(("gx", "gy"), None, None),
        check_vma=False,
    )
```

```python
import functools

import jax
import jax.numpy as jnp
from jax import lax
from jax.experimental import pallas as pl
from jax.experimental.pallas import tpu as pltpu
from jax.sharding import PartitionSpec as P

BF = jnp.bfloat16
F32 = jnp.float32
DOF = 384
FDOF = 96
CDOF = 48
LANES = 128
E_DEV = 8
CITER = 4
KLOC = 768
KREM = 256
relax_fine = 0.7
relax_coarse = 0.5


def mm(a, b):
    return jnp.dot(a, b, preferred_element_type=F32)


WHOLE = (pl.ds(0, DOF),)
HALVES = (pl.ds(0, DOF // 2), pl.ds(DOF // 2, DOF // 2))


def x_trace(ref, node):
    return ref[pl.ds(node, FDOF, stride=4), :]


def y_trace(value, node):
    tiles = value.reshape(12, 4, 8, LANES)
    upper = lax.broadcasted_iota(jnp.int32, (12, 8, LANES), 1) < 4
    if node == 0:
        low, high = tiles[:, 0], pltpu.roll(tiles[:, 2], 4, axis=1)
    else:
        low, high = pltpu.roll(tiles[:, 1], 4, axis=1), tiles[:, 3]
    return jnp.where(upper, low, high).reshape(FDOF, LANES)


def z_trace(value, node):
    return value.reshape(6, 4, 16, LANES)[:, node].reshape(FDOF, LANES)


def kernel(
    n_gx, n_gy,
    rhs_h, diag_h, inv_h, coup_h, prol_h, face_h, sub_h,
    out_v,
    rhs_v, inv_v, face_t, w_all, stack, x_v, r_v, rb_v,
    prol_f, prol_b, prol_t, prol_face, send_b, near,
    rest_v, block_v, stiff_v, part_m, part_r, pair_m, pair_r, chip_m, chip_r, got_m, got_r, y_all, share_s, face_s, sub_s,
    inv_sem, load_sem, halo_send, halo_recv, pair_send, pair_recv, ring_send, ring_recv, y_recv,
):
    gx = lax.axis_index("gx")
    gy = lax.axis_index("gy")
    west, east = lax.rem(gx + n_gx - 1, n_gx), lax.rem(gx + 1, n_gx)
    south, north = lax.rem(gy + n_gy - 1, n_gy), lax.rem(gy + 1, n_gy)
    core, z, n_z = lax.rem(gy, 2), gy // 2, n_gy // 2
    sibling = gy + 1 - 2 * core
    hops = sorted(range(1, n_z), key=lambda d: -min(d, n_z - d))
    row_partners = sorted({1, n_gy - 1} | {2 * d for d in hops}, key=lambda t: -min(t, n_gy - t))
    half = E_DEV // 2

    inv_loads = [pltpu.make_async_copy(inv_h.at[e], inv_v.at[e], inv_sem.at[e]) for e in range(E_DEV)]
    first_part, rest_part = pl.ds(0, 1), pl.ds(1, E_DEV - 1)
    rhs_loads = [
        pltpu.make_async_copy(rhs_h.at[part], rhs_v.at[part], load_sem.at[g])
        for g, part in enumerate((first_part, rest_part))
    ]
    late_loads = [
        pltpu.make_async_copy(prol_h, prol_t, load_sem.at[2]),
        pltpu.make_async_copy(face_h, face_s, load_sem.at[9]),
        pltpu.make_async_copy(sub_h, sub_s, load_sem.at[10]),
    ]
    for g in range(2):
        part = pl.ds(g * half, half)
        late_loads += [
            pltpu.make_async_copy(coup_h.at[part, pl.ds(0, 4)], face_t.at[part, pl.ds(0, 4)], load_sem.at[3 + g]),
            pltpu.make_async_copy(coup_h.at[part, 5 - g], face_t.at[part, 4], load_sem.at[5 + g]),
            pltpu.make_async_copy(diag_h.at[part], w_all.at[part, :, pl.ds(0, DOF)], load_sem.at[7 + g]),
        ]
    barrier = pltpu.get_barrier_semaphore()
    for t in row_partners:
        pl.semaphore_signal(
            barrier, inc=1, device_id={"gy": lax.rem(gy + t, n_gy)}, device_id_type=pl.DeviceIdType.MESH
        )
    for other in (west, east):
        pl.semaphore_signal(barrier, inc=1, device_id={"gx": other}, device_id_type=pl.DeviceIdType.MESH)

    inv_loads[0].start()
    rhs_loads[0].start()
    rhs_loads[1].start()
    for copy in inv_loads[1:]:
        copy.start()

    def halo(h, e):
        i, j = e % 2, e // 2 % 2
        x_to, y_to = (west, east)[i], (south, north)[j]
        x_pair, y_pair = e + 1 - 2 * i, e + 2 - 4 * j
        return (
            pltpu.make_async_remote_copy(
                src_ref=send_b.at[h, e, 0],
                dst_ref=near.at[h, x_pair, pl.ds(0, FDOF)],
                send_sem=halo_send.at[h],
                recv_sem=halo_recv.at[h, x_pair],
                device_id={"gx": x_to},
                device_id_type=pl.DeviceIdType.MESH,
            ),
            pltpu.make_async_remote_copy(
                src_ref=send_b.at[h, e, 1],
                dst_ref=near.at[h, y_pair, pl.ds(FDOF, FDOF)],
                send_sem=halo_send.at[h],
                recv_sem=halo_recv.at[h, y_pair],
                device_id={"gy": y_to},
                device_id_type=pl.DeviceIdType.MESH,
            ),
        )

    def halo_arrived(h, e):
        pltpu.make_async_copy(near.at[h, e], near.at[h, e], halo_recv.at[h, e]).wait()

    def publish(h, e):
        i, j = e % 2, e // 2 % 2
        ref = x_v.at[e]
        value = ref[...]
        send_b[h, e, 0] = x_trace(ref, 3 * i).astype(BF)
        send_b[h, e, 1] = y_trace(value, 3 * j).astype(BF)

    def settle(e):
        i, j, k = e % 2, e // 2 % 2, e // 4
        ref = x_v.at[e]
        value = ref[...]
        stack[e, pl.ds(0, DOF), :] = value.astype(BF)
        stack[e + 4 - 8 * k, pl.ds(384, FDOF), :] = z_trace(value, 3 - 3 * k).astype(BF)
        stack[e + 1 - 2 * i, pl.ds(512, FDOF), :] = x_trace(ref, 3 - 3 * i).astype(BF)
        stack[e + 2 - 4 * j, pl.ds(608, FDOF), :] = y_trace(value, 3 - 3 * j).astype(BF)

    def launch(h, e):
        for copy in halo(h, e):
            copy.start()

    for e in range(E_DEV):
        stack[e, pl.ds(480, 32), :] = jnp.zeros((32, LANES), BF)
        stack[e, pl.ds(704, 64), :] = jnp.zeros((64, LANES), BF)

    for t in range(E_DEV + 1):
        if t < E_DEV:
            inv_loads[t].wait()
            if t < 2:
                rhs_loads[t].wait()
        if t >= 1:
            publish(0, t - 1)
        if t < E_DEV:
            for rows in HALVES:
                x_v[t, rows, :] = relax_fine * mm(inv_v[t, rows, :], rhs_v[t])
        if t == 3:
            for copy in late_loads:
                copy.start()
        if t == 3:
            pl.semaphore_wait(barrier, len(row_partners) + 2)
            for face in range(2):
                for e in range(3):
                    halo(0, e)[face].start()
        if t > 3:
            launch(0, t - 1)

    for e in range(E_DEV):
        settle(e)
    for copy in late_loads:
        copy.wait()
    for s in range(n_gy):
        for e in range(E_DEV):
            share_s[s, e] = (sub_s[e] == s).astype(F32)
    prol_pad = jnp.concatenate([prol_t[...].astype(F32), jnp.zeros((LANES - CDOF, DOF), F32)], axis=0)
    prol_full = jnp.transpose(prol_pad)
    prol_f[...] = prol_full
    prol_b[...] = prol_full.astype(BF)
    for node in range(2):
        prol_face[0 + 1 - node] = x_trace(prol_f, 3 * node).astype(BF)
        prol_face[2 + 1 - node] = y_trace(prol_full, 3 * node).astype(BF)
        prol_face[4 + 1 - node] = z_trace(prol_full, 3 * node).astype(BF)

    zeros_32 = jnp.zeros((32, LANES), BF)
    zeros_64 = jnp.zeros((64, LANES), BF)
    one_at = (lax.broadcasted_iota(jnp.int32, (CDOF // 2, LANES), 1) == 2 * CDOF).astype(F32)

    def pack(e):
        i, j, k = e % 2, e // 2 % 2, e // 4

        def face(f):
            live = (face_s[e, f] > 0).astype(F32).astype(BF)
            return face_t[e, min(f, 4)] * live

        pad_32, pad_64 = jnp.zeros((32, DOF), BF), jnp.zeros((64, DOF), BF)
        z_part = jnp.concatenate([face(5 - k), pad_32], axis=0)
        near_part = jnp.concatenate([face(1 - i), face(3 - j), pad_64], axis=0)
        far_part = jnp.concatenate([face(i), face(2 + j), pad_64], axis=0)
        w_all[e, :, pl.ds(DOF, 128)] = jnp.transpose(z_part)
        w_all[e, :, pl.ds(512, 256)] = jnp.transpose(near_part)
        w_all[e, :, pl.ds(KLOC, KREM)] = jnp.transpose(far_part)

    def local_both(e):
        i, j, k = e % 2, e // 2 % 2, e // 4
        prol_stack = jnp.concatenate(
            [
                prol_b[...], prol_face[5 - k], zeros_32, prol_face[1 - i], prol_face[3 - j], zeros_64,
                prol_face[i], prol_face[2 + j], zeros_64,
            ],
            axis=0,
        )
        state = jnp.concatenate([stack[e], jnp.zeros((KREM, LANES), BF)], axis=0)
        for rows in HALVES:
            both = mm(w_all[e, rows, :], jnp.concatenate([state, prol_stack], axis=1))
            r_v[e, rows, :] = rhs_v[e, rows, :].astype(F32) - both[:, :LANES]
            stiff_v[e, rows, :] = both[:, LANES:].astype(BF)

    for t in range(E_DEV + 2):
        if t < E_DEV:
            pack(t)
        if 1 <= t <= E_DEV:
            local_both(t - 1)
        if t >= 2:
            block = mm(prol_t[...], stiff_v[t - 2])
            block_v[t - 2] = block[:CDOF // 2] + pltpu.roll(block[CDOF // 2:], CDOF, axis=1) + one_at

    def spread(part, source, size):
        for c in range(source.shape[1] // size):
            rows = pl.ds(c * size, size)
            pieces = [source[e, rows, :] for e in range(E_DEV)]
            for s in range(n_gy):
                total = share_s[s, 0] * pieces[0]
                for e in range(1, E_DEV):
                    total = total + share_s[s, e] * pieces[e]
                part[s % 2, s // 2, rows, :] = total.astype(BF)

    def remote(to, src, dst, send_sem, recv_sem):
        return pltpu.make_async_remote_copy(
            src_ref=src,
            dst_ref=dst,
            send_sem=send_sem,
            recv_sem=recv_sem,
            device_id={"gy": to},
            device_id_type=pl.DeviceIdType.MESH,
        )

    def same_core(d):
        return 2 * lax.rem(z + d, n_z) + core

    def pair_copy(c, part, pair):
        return remote(sibling, part.at[1 - core], pair, pair_send.at[c], pair_recv.at[c])

    def scatter(c, part, pair, chip, got):
        pair_copy(c, part, pair).wait_recv()
        for at in range(n_z):
            chip[at] = (part[core, at].astype(F32) + pair[at].astype(F32)).astype(BF)
        for d in hops:
            remote(
                same_core(d), chip.at[lax.rem(z + d, n_z)], got.at[d - 1], ring_send.at[c], ring_recv.at[c]
            ).start()

    def all_of(got, sem):
        return pltpu.make_async_copy(got, got, sem)

    def gathered_sum(c, part, pair, got):
        total = part[core, z].astype(F32) + pair[z].astype(F32)
        if n_z > 1:
            all_of(got, ring_recv.at[c]).wait()
            for d in hops:
                total = total + got[d - 1].astype(F32)
        return total

    spread(part_m, block_v, CDOF // 2)
    pair_copy(0, part_m, pair_m).start()

    def residual(h, e):
        far = jnp.concatenate([near[h, e], zeros_64], axis=0)
        for rows in HALVES:
            rb_v[e, rows, :] = (r_v[e, rows, :] - mm(w_all[e, rows, pl.ds(KLOC, KREM)], far)).astype(BF)

    for t in range(E_DEV + 1):
        if t < E_DEV:
            halo_arrived(0, t)
            residual(0, t)
        if t >= 1:
            rest_v[t - 1] = mm(prol_t[...], rb_v[t - 1])
    spread(part_r, rest_v, 16)
    pair_copy(1, part_r, pair_r).start()
    scatter(0, part_m, pair_m, chip_m, got_m)
    scatter(1, part_r, pair_r, chip_r, got_r)

    matrix_sum = gathered_sum(0, part_m, pair_m, got_m)
    matrix = jnp.concatenate(
        [matrix_sum[:, :CDOF], pltpu.roll(matrix_sum, LANES - CDOF, axis=1)[:, :CDOF]], axis=0
    )
    matrix_high = matrix.astype(BF)
    matrix_low = (matrix - matrix_high.astype(F32)).astype(BF)
    matrix_parts = jnp.concatenate([matrix_high, matrix_high, matrix_low], axis=1)
    theta = relax_coarse / jnp.maximum(matrix_sum[:1, 2 * CDOF:2 * CDOF + 1], 1.0)
    coarse_rhs = gathered_sum(1, part_r, pair_r, got_r)
    coarse = theta * coarse_rhs
    for sweep in range(CITER - 1):
        high = coarse.astype(BF)
        low = (coarse - high.astype(F32)).astype(BF)
        applied = mm(matrix_parts, jnp.concatenate([high, low, high], axis=0))
        coarse = coarse + theta * (coarse_rhs - applied)
    y_all[gy] = coarse.astype(BF)
    for d in hops:
        remote(same_core(d), y_all.at[gy], y_all.at[gy], ring_send.at[2], y_recv.at[d]).start()
    remote(sibling, y_all.at[gy], y_all.at[gy], pair_send.at[2], pair_recv.at[2]).start()
    pltpu.make_async_copy(send_b.at[0], send_b.at[0], halo_send.at[0]).wait()
    for c, part in ((0, part_m), (1, part_r)):
        all_of(part.at[0], pair_send.at[c]).wait()
    if n_z > 1:
        all_of(got_m, ring_send.at[0]).wait()
        all_of(got_r, ring_send.at[1]).wait()
    for d in reversed(hops):
        came = same_core(n_z - d)
        remote(sibling, y_all.at[came], y_all.at[came], pair_send.at[2], y_recv.at[d]).wait_recv()
        remote(sibling, y_all.at[came], y_all.at[came], pair_send.at[2], pair_recv.at[2]).start()
    all_of(part_r.at[0], pair_recv.at[2]).wait()

    zeros_80 = jnp.zeros((LANES - CDOF, LANES), BF)
    for t in range(E_DEV + 1):
        if t >= 1:
            publish(1, t - 1)
        if t < E_DEV:
            picked = jnp.concatenate([y_all[sub_s[t]], zeros_80], axis=0)
            for rows in HALVES:
                x_v[t, rows, :] = x_v[t, rows, :] + mm(prol_b[rows, :], picked)
        if t >= 1:
            launch(1, t - 1)

    for h in (1, 2):
        for e in range(E_DEV):
            settle(e)
        for e in range(E_DEV):
            for rows in WHOLE:
                r_v[e, rows, :] = rhs_v[e, rows, :].astype(F32) - mm(w_all[e, rows, pl.ds(0, KLOC)], stack[e])
        if h == 2:
            pltpu.make_async_copy(send_b.at[1], send_b.at[1], halo_send.at[1]).wait()
            all_of(part_r.at[0], pair_send.at[2]).wait()
            if n_z > 1:
                all_of(got_r, ring_send.at[2]).wait()
        for t in range(E_DEV + 2):
            if t < E_DEV:
                halo_arrived(h, t)
            if t >= 2 and h == 1:
                publish(2, t - 2)
            if t < E_DEV:
                residual(h, t)
            if 1 <= t <= E_DEV:
                target = x_v if h == 1 else out_v
                for rows in HALVES:
                    target[t - 1, rows, :] = x_v[t - 1, rows, :] + relax_fine * mm(inv_v[t - 1, rows, :], rb_v[t - 1])
            if t >= 2 and h == 1:
                launch(2, t - 2)
    pltpu.make_async_copy(send_b.at[2], send_b.at[2], halo_send.at[2]).wait()


def on_device(n_gx, n_gy, rhs, diag_blocks, inverse_blocks, couplings, prolong, face_source, subset):
    any_space = pl.BlockSpec(memory_space=pl.ANY)
    dma = pltpu.SemaphoreType.DMA
    n_z = n_gy // 2
    return pl.pallas_call(
        functools.partial(kernel, n_gx, n_gy),
        out_shape=pltpu.VMEM((E_DEV, DOF, LANES), F32),
        in_specs=[any_space] * 7,
        out_specs=pl.BlockSpec(memory_space=pltpu.VMEM),
        scratch_shapes=[
            pltpu.VMEM((E_DEV, DOF, LANES), BF),
            pltpu.VMEM((E_DEV, DOF, DOF), BF),
            pltpu.VMEM((E_DEV, 5, FDOF, DOF), BF),
            pltpu.VMEM((E_DEV, DOF, KLOC + KREM), BF),
            pltpu.VMEM((E_DEV, KLOC, LANES), BF),
            pltpu.VMEM((E_DEV, DOF, LANES), F32),
            pltpu.VMEM((E_DEV, DOF, LANES), F32),
            pltpu.VMEM((E_DEV, DOF, LANES), BF),
            pltpu.VMEM((DOF, LANES), F32),
            pltpu.VMEM((DOF, LANES), BF),
            pltpu.VMEM((CDOF, DOF), BF),
            pltpu.VMEM((6, FDOF, LANES), BF),
            pltpu.VMEM((3, E_DEV, 2, FDOF, LANES), BF),
            pltpu.VMEM((3, E_DEV, 2 * FDOF, LANES), BF),
            pltpu.VMEM((E_DEV, CDOF, LANES), F32),
            pltpu.VMEM((E_DEV, CDOF // 2, LANES), F32),
            pltpu.VMEM((E_DEV, DOF, LANES), BF),
            pltpu.VMEM((2, n_z, CDOF // 2, LANES), BF),
            pltpu.VMEM((2, n_z, CDOF, LANES), BF),
            pltpu.VMEM((n_z, CDOF // 2, LANES), BF),
            pltpu.VMEM((n_z, CDOF, LANES), BF),
            pltpu.VMEM((n_z, CDOF // 2, LANES), BF),
            pltpu.VMEM((n_z, CDOF, LANES), BF),
            pltpu.VMEM((max(n_z - 1, 1), CDOF // 2, LANES), BF),
            pltpu.VMEM((max(n_z - 1, 1), CDOF, LANES), BF),
            pltpu.VMEM((n_gy, CDOF, LANES), BF),
            pltpu.SMEM((n_gy, E_DEV), F32),
            pltpu.SMEM((E_DEV, 6), jnp.int32),
            pltpu.SMEM((E_DEV,), jnp.int32),
            dma((E_DEV,)),
            dma((11,)),
            dma((3,)),
            dma((3, E_DEV)),
            dma((3,)),
            dma((3,)),
            dma((3,)),
            dma((2,)),
            dma((n_z,)),
        ],
        compiler_params=pltpu.CompilerParams(
            collective_id=0, has_side_effects=True, vmem_limit_bytes=56 * 1024 * 1024
        ),
    )(rhs, diag_blocks, inverse_blocks, jnp.swapaxes(couplings, 2, 3), prolong.T, face_source, subset)


def solution(mesh):
    return jax.shard_map(
        functools.partial(on_device, mesh.shape["gx"], mesh.shape["gy"]),
        mesh=mesh,
        in_specs=(
            P(("gx", "gy"), None, None),
            P(("gx", "gy"), None, None),
            P(("gx", "gy"), None, None),
            P(("gx", "gy"), None, None, None),
            P(),
            P(("gx", "gy"), None),
            P(("gx", "gy")),
        ),
        out_specs=P(("gx", "gy"), None, None),
        check_vma=False,
    )
```
